32 devices in a mesh: expert: 8 (over z, y), mirror: 4 (over x, core).
Axes of the slice: x: 2, y: 2, z: 4, core: 2. Of those that a mesh axis runs over, the one named last changes fastest.
Arguments:
- out_grad: bfloat16 [8, 4, 2, 96, 2048], P('expert', 'mirror'), may hold values from -6 to 6
- gate_prob: float32 [8, 4, 2, 96], P('expert', 'mirror'), may hold values from 0.1 to 1
- dest_expert: int32 [8, 4, 2, 96], P('expert', 'mirror'), may hold values from 0 to 7, as said below
- dest_slot: int32 [8, 4, 2, 96], P('expert', 'mirror'), may hold values from 0 to 31, as said below
- x_saved: bfloat16 [8, 4, 2, 256, 2048], P('expert', 'mirror'), may hold values from -6 to 6
- w_gate_up: bfloat16 [8, 2048, 512], P('expert', 'mirror'), may hold values from -0.125 to 0.125
- w_down: bfloat16 [8, 256, 2048], P('expert', 'mirror'), may hold values from -0.375 to 0.375
Outputs:
- in_grad: bfloat16 [8, 4, 2, 96, 2048], P('expert', 'mirror')
- grad_gate_up: bfloat16 [8, 2048, 512], P('expert', 'mirror')
- grad_down: bfloat16 [8, 256, 2048], P('expert', 'mirror')
The draws below stay inside these ranges and needn't reach their ends.
Inputs may be any that keep to these rules, and one draw needn't show every extreme that they name: `dest_expert`: rows of one device in one microbatch name no expert more than 32 times. `dest_slot`: rows of one device in one microbatch that name the same expert have different slots.
All inputs are finite; a program needn't handle non-finite values.
Results may differ from the reference program's by a relative error of at most 0.0095.
Values may be sent and summed in bfloat16 or wider, within the bound.
No kernel may reach another device: no remote copies, remote signals or barrier semaphores. Data moves between devices by JAX's collectives and lax.ppermute only.
A program may use at most 64 MiB of HBM per device.

```python
import jax
import jax.numpy as jnp
from jax import lax

D = 2048
F = 256
MICRO = 2
ROWS = 96
EXPERTS = 8
PEER = 32
CAP = 256
N_EXPERT = 8
N_MIRROR = 4


def route_ids(key):
    base_key = jax.random.fold_in(key, 7)
    id_count = N_EXPERT * PEER
    block_total = N_EXPERT * N_MIRROR * MICRO

    def one_block(block_index):
        micro_index = block_index % MICRO
        mirror_index = block_index // MICRO % N_MIRROR
        group_key = jax.random.fold_in(base_key, 100000 + mirror_index * MICRO + micro_index)
        forced = jax.random.randint(group_key, (), 0, N_EXPERT)
        block_key = jax.random.fold_in(base_key, block_index)
        ranking = jax.random.permutation(jax.random.fold_in(block_key, 1), id_count).astype(jnp.int32)
        id_values = jnp.arange(id_count, dtype=jnp.int32)
        sort_score = ranking + id_count * (id_values // PEER != forced).astype(jnp.int32)
        ordering = jnp.argsort(sort_score)
        chosen = ordering[:ROWS].astype(jnp.int32)
        return jax.random.permutation(jax.random.fold_in(block_key, 2), chosen)
    route_table = jax.vmap(one_block)(jnp.arange(block_total, dtype=jnp.int32))
    return route_table.reshape(N_EXPERT, N_MIRROR, MICRO, ROWS)


def draw_dest_expert(key, part):
    return route_ids(key) // PEER


def draw_dest_slot(key, part):
    return route_ids(key) % PEER


def block_levels(rng, extent, cuts, smallest, largest):
    def one(position, parts):
        draws = jax.random.uniform(jax.random.fold_in(jax.random.fold_in(rng, 6), position), (parts,), jnp.float32, smallest / len(cuts), largest / len(cuts))
        return jnp.repeat(jnp.exp(draws), extent[position] // parts).reshape((-1,) + (1,) * (len(extent) - position - 1))

    level = one(*cuts[0])
    for cut in cuts[1:]:
        level = level * one(*cut)
    return level


def noise(own_key, shape, deviation, most, pieces=(), held_as=jnp.bfloat16):
    gain = block_levels(own_key, shape, pieces, -0.22, 0.18) if pieces else 1.0
    array = jax.random.normal(own_key, shape, jnp.float32) * deviation * gain
    return jnp.minimum(jnp.maximum(array, -most), most).astype(held_as)


def setup_inputs(seed: int = 0) -> dict:
    key_list = jax.random.split(jax.random.key(seed), 8)
    out_grad = noise(key_list[0], (EXPERTS, N_MIRROR, MICRO, ROWS, D), 1.0, 6.0, ((0, 8), (1, 4)))
    gate_prob = jnp.clip(0.1 + 0.9 * jax.random.uniform(key_list[1], (EXPERTS, N_MIRROR, MICRO, ROWS), jnp.float32) ** block_levels(key_list[1], (EXPERTS, N_MIRROR, MICRO, ROWS), ((0, 8), (1, 4)), -0.2, 0.2), 0.1, 1.0)
    dest_expert = draw_dest_expert(jax.random.fold_in(key_list[7], 71), 0)
    dest_slot = draw_dest_slot(jax.random.fold_in(key_list[7], 71), 0)
    x_saved = noise(key_list[4], (EXPERTS, N_MIRROR, MICRO, CAP, D), 1.0, 6.0, ((0, 8), (1, 4)))
    w_gate_up = noise(key_list[5], (EXPERTS, D, 2 * F), D ** -0.5, 0.125, ((0, 8), (1, 4)))
    w_down = noise(key_list[6], (EXPERTS, F, D), F ** -0.5, 0.375, ((0, 8), (1, 4)))
    return {"out_grad": out_grad, "gate_prob": gate_prob, "dest_expert": dest_expert, "dest_slot": dest_slot, "x_saved": x_saved, "w_gate_up": w_gate_up, "w_down": w_down}


def silu_parts(values):
    sigmoid_vals = jax.nn.sigmoid(values)
    return values * sigmoid_vals, sigmoid_vals * (1.0 + values * (1.0 - sigmoid_vals))


def expert_pass(inputs, grad_rows, w_gate_up_e, w_down_e):
    gate_up = jnp.dot(inputs, w_gate_up_e, preferred_element_type=jnp.float32)
    gate_part = gate_up[:, :F]
    up_part = gate_up[:, F:]
    activation, slope_term = silu_parts(gate_part)
    hidden = (activation * up_part).astype(jnp.bfloat16)
    unit_grad = jnp.dot(grad_rows, w_down_e.T, preferred_element_type=jnp.float32)
    gate_up_grad = jnp.concatenate([unit_grad * up_part * slope_term, unit_grad * activation], axis=1).astype(jnp.bfloat16)
    slot_input_grad = jnp.dot(gate_up_grad, w_gate_up_e.T, preferred_element_type=jnp.float32).astype(jnp.bfloat16)
    part_gate_up = jnp.dot(inputs.T, gate_up_grad, preferred_element_type=jnp.float32).astype(jnp.bfloat16)
    part_down = jnp.dot(hidden.T, grad_rows, preferred_element_type=jnp.float32).astype(jnp.bfloat16)
    return slot_input_grad, part_gate_up, part_down


def reference(out_grad, gate_prob, dest_expert, dest_slot, x_saved, w_gate_up, w_down):
    weighted = (out_grad.astype(jnp.float32) * gate_prob[..., None]).astype(jnp.bfloat16)
    source = jnp.arange(EXPERTS, dtype=jnp.int32)[:, None, None, None]
    mirror_idx = jnp.arange(N_MIRROR, dtype=jnp.int32)[None, :, None, None]
    micro_idx = jnp.arange(MICRO, dtype=jnp.int32)[None, None, :, None]
    column = (source * PEER + dest_slot).astype(jnp.int32)
    slot_grad = jnp.zeros((EXPERTS, N_MIRROR, MICRO, CAP, D), jnp.bfloat16)
    slot_grad = slot_grad.at[dest_expert, mirror_idx, micro_idx, column].set(weighted)

    def per_expert(operands):
        inputs_e, grads_e, w_gu_e, w_down_e = operands

        def per_rank(rank_pair):
            inputs_m, grads_m = rank_pair
            slot_input_grad, part_gu, part_down = expert_pass(
                inputs_m.reshape(MICRO * CAP, D), grads_m.reshape(MICRO * CAP, D), w_gu_e, w_down_e)
            part_gu, part_down = lax.optimization_barrier((part_gu, part_down))
            return slot_input_grad.reshape(MICRO, CAP, D), part_gu, part_down

        slot_input_grad, parts_gu, parts_down = lax.map(per_rank, (inputs_e, grads_e))
        summed_gu = jnp.sum(parts_gu.astype(jnp.float32), axis=0).astype(jnp.bfloat16)
        summed_down = jnp.sum(parts_down.astype(jnp.float32), axis=0).astype(jnp.bfloat16)
        return slot_input_grad, summed_gu, summed_down

    slot_input_grad, grad_gate_up, grad_down = lax.map(per_expert, (x_saved, slot_grad, w_gate_up, w_down))
    in_grad = slot_input_grad[dest_expert, mirror_idx, micro_idx, column]
    return (in_grad, grad_gate_up, grad_down)
```

```python
import jax
import jax.numpy as jnp
from jax import lax
from jax.experimental import pallas as pl
from jax.experimental.pallas import tpu as pltpu
from jax.sharding import PartitionSpec as P


BF16 = jnp.bfloat16
F32 = jnp.float32
VMEM_LIMIT = 12 * 1024 * 1024


def copied_spec(shape):
    zeros = (0,) * len(shape)
    return pl.BlockSpec(tuple(shape), lambda i: zeros)


def resident_spec():
    return pl.BlockSpec(memory_space=pltpu.VMEM)


def call(body, operands, out_shapes, flops=0, scratch=(), in_specs=None, out_specs=None, aliases=None, steps=1, exps=0):
    shapes = [jax.ShapeDtypeStruct(shape, dtype) for shape, dtype in out_shapes]
    moved = sum(v.size * v.dtype.itemsize for v in (*operands, *shapes))
    return pl.pallas_call(
        body,
        grid=(steps,),
        in_specs=in_specs or [resident_spec()] * len(operands),
        out_specs=out_specs or [resident_spec()] * len(shapes),
        out_shape=shapes,
        scratch_shapes=list(scratch),
        input_output_aliases=aliases or {},
        compiler_params=pltpu.CompilerParams(vmem_limit_bytes=VMEM_LIMIT),
        cost_estimate=pl.CostEstimate(flops=flops, bytes_accessed=moved, transcendentals=exps),
    )(*operands)


def dot_nt(left_side, right_side):
    return lax.dot_general(
        left_side, right_side, (((1,), (1,)), ((), ())), preferred_element_type=F32
    )


def dot_tn(left_side, right_side):
    return lax.dot_general(
        left_side, right_side, (((0,), (0,)), ((), ())), preferred_element_type=F32
    )


def silu_parts(values):
    sigmoid_vals = jax.nn.sigmoid(values)
    return (values * sigmoid_vals, sigmoid_vals * (1.0 + values * (1.0 - sigmoid_vals)))


def swap(value, axis, bit):
    size = lax.axis_size(axis)
    return lax.ppermute(value, axis, [(i, i ^ bit) for i in range(size)])


def as_column(row):
    count = row.shape[1]
    down = lax.broadcasted_iota(jnp.int32, (count, count), 0)
    across = lax.broadcasted_iota(jnp.int32, (count, count), 1)
    spread = jnp.broadcast_to(row, (count, count))
    return jnp.sum(jnp.where(down == across, spread, jnp.zeros_like(spread)), axis=1, keepdims=True)


def relative_position(expert_ref, slot_ref, b, peer_slots, relative):
    expert_row = expert_ref[b : b + 1, :]
    if relative:
        expert_row = expert_row ^ lax.axis_index("expert")
    return expert_row * peer_slots + slot_ref[b : b + 1, :]


STEP = 512


def place_rows(out_grad, gate_prob, dest_expert, dest_slot, b, n_expert, peer_slots, relative, after):
    rows, width = out_grad.shape[1:]
    capacity = n_expert * peer_slots
    operands = [out_grad, gate_prob, dest_expert, dest_slot]
    in_specs = [pl.BlockSpec((1, rows, width), lambda i: (b, 0, 0))]
    in_specs += [copied_spec(v.shape) for v in operands[1:]]
    if after is not None:
        operands.append(after)
        in_specs.append(pl.BlockSpec(memory_space=pl.ANY))

    def body(grad_ref, prob_ref, expert_ref, slot_ref, *refs):
        out_refs = refs[-count:]
        position = relative_position(expert_ref, slot_ref, b, peer_slots, relative)
        slot_ids = lax.broadcasted_iota(jnp.int32, (capacity, rows), 0)
        placing = jnp.where(slot_ids == position, 1.0, 0.0).astype(BF16)
        prob = as_column(prob_ref[b : b + 1, :])
        for start in range(0, width, STEP):
            columns = slice(start, start + STEP)
            weighted = (grad_ref[0, :, columns].astype(F32) * prob).astype(BF16)
            slots = jnp.dot(placing, weighted, preferred_element_type=F32).astype(BF16)
            if relative:
                for k in range(n_expert):
                    out_refs[k][:, columns] = slots[k * peer_slots : (k + 1) * peer_slots]
            else:
                out_refs[0][:, columns] = slots

    count, block_rows = (n_expert, peer_slots) if relative else (1, capacity)
    return call(
        body,
        operands,
        [((block_rows, width), BF16)] * count,
        flops=2 * capacity * rows * width,
        in_specs=in_specs,
    )


def prepare(pieces_gu, pieces_down, saved):
    rows_gu, both = pieces_gu[0].shape
    rows_down, width = pieces_down[0].shape
    count = len(pieces_gu)
    slots = saved.shape[0]

    def body(*refs):
        mine = lax.axis_index("mirror")
        saved_ref = refs[2 * count]
        gu_ref, down_ref, gate_up_ref = refs[2 * count + 1 :]
        total = None
        for j in range(count):
            at = pl.ds(pl.multiple_of((mine ^ j) * rows_gu, rows_gu), rows_gu)
            gu_ref[at, :] = refs[j][...]
            term = jnp.dot(saved_ref[:, at], refs[j][...], preferred_element_type=F32)
            total = term if total is None else total + term
            down = pl.ds(pl.multiple_of((mine ^ j) * rows_down, rows_down), rows_down)
            down_ref[down, :] = refs[count + j][...]
        gate_up_ref[...] = total

    return call(
        body,
        [*pieces_gu, *pieces_down, saved],
        [((count * rows_gu, both), BF16), ((count * rows_down, width), BF16), ((slots, both), F32)],
        flops=2 * slots * width * both,
    )


def expert_rows(arrived, gate_up, full_gu, full_down, b, n_expert, relative):
    both = gate_up.shape[1]
    hidden_units = both // 2
    width = full_gu.shape[0]
    count = len(arrived)
    peer_slots = arrived[0].shape[0] if relative else arrived[0].shape[0] // n_expert
    capacity = n_expert * peer_slots

    def body(*refs):
        blocks = refs[:count]
        gate_up_ref, gu_ref, down_ref = refs[count : count + 3]
        rows_refs = refs[count + 3 : 2 * count + 3]
        grad_ref, hidden_ref = refs[2 * count + 3 : 2 * count + 5]
        if relative:
            slots_ref, stage = refs[2 * count + 5 :]
            me = lax.axis_index("expert")
            spots = [
                pl.ds(pl.multiple_of((me ^ k) * peer_slots, peer_slots), peer_slots)
                for k in range(n_expert)
            ]
            for k in range(n_expert):
                slots_ref[spots[k], :] = blocks[k][...]
            unit_grad = dot_nt(slots_ref[...], down_ref[...])
        else:
            unit_grad = dot_nt(blocks[0][...], down_ref[...])
        mine = slice(b * capacity, (b + 1) * capacity)
        gate_part = gate_up_ref[mine, :hidden_units]
        up_part = gate_up_ref[mine, hidden_units:]
        activation, slope_term = silu_parts(gate_part)
        hidden_ref[...] = (activation * up_part).astype(BF16)
        grad_ref[:, :hidden_units] = (unit_grad * up_part * slope_term).astype(BF16)
        grad_ref[:, hidden_units:] = (unit_grad * activation).astype(BF16)
        for start in range(0, width, STEP):
            rows = dot_nt(grad_ref[...], gu_ref[start : start + STEP, :]).astype(BF16)
            if relative:
                stage[:, start : start + STEP] = rows
            else:
                rows_refs[0][:, start : start + STEP] = rows
        if relative:
            for k in range(n_expert):
                rows_refs[k][...] = stage[spots[k], :]

    out_shapes = [(arrived[0].shape, BF16)] * count
    out_shapes += [((capacity, both), BF16), ((capacity, hidden_units), BF16)]
    if relative:
        out_shapes.append(((capacity, width), BF16))
    operands = [*arrived, gate_up, full_gu, full_down]
    return call(
        body,
        operands,
        out_shapes,
        flops=2 * capacity * width * (both + hidden_units),
        exps=capacity * hidden_units,
        scratch=[pltpu.VMEM((capacity, width), BF16)] if relative else [],
    )


def unplace_rows(back, dest_expert, dest_slot, b, n_expert, relative, rows, previous, micro_count):
    width = back[0].shape[1]
    count = len(back)
    peer_slots = back[0].shape[0] if relative else back[0].shape[0] // n_expert
    capacity = n_expert * peer_slots

    def body(*refs):
        expert_ref, slot_ref = refs[:2]
        blocks = refs[2 : 2 + count]
        out_ref = refs[-2] if relative else refs[-1]
        position = as_column(relative_position(expert_ref, slot_ref, b, peer_slots, relative))
        slot_ids = lax.broadcasted_iota(jnp.int32, (rows, capacity), 1)
        taking = jnp.where(slot_ids == position, 1.0, 0.0).astype(BF16)
        if relative:
            stage = refs[-1]
            for k in range(n_expert):
                stage[k * peer_slots : (k + 1) * peer_slots, :] = blocks[k][...]
        else:
            stage = blocks[0]
        for start in range(0, width, STEP):
            columns = slice(start, start + STEP)
            out_ref[0, :, columns] = jnp.dot(
                taking, stage[:, columns], preferred_element_type=F32
            ).astype(BF16)

    operands = [dest_expert, dest_slot, *back]
    in_specs = [copied_spec(v.shape) for v in operands[:2]] + [resident_spec()] * count
    aliases = {}
    if previous is not None:
        aliases = {len(operands): 0}
        operands.append(previous)
        in_specs.append(pl.BlockSpec(memory_space=pl.ANY))
    return call(
        body,
        operands,
        [((micro_count, rows, width), BF16)],
        flops=2 * capacity * rows * width,
        in_specs=in_specs,
        out_specs=[pl.BlockSpec((1, rows, width), lambda i: (b, 0, 0))],
        scratch=[pltpu.VMEM((capacity, width), BF16)] if relative else [],
        aliases=aliases,
    )[0]


def weight_parts(saved, grads, hidden, slots):
    micro_count = len(grads)
    capacity, both = grads[0].shape
    hidden_units = hidden[0].shape[1]
    width = saved.shape[1]
    rows_gu, rows_down = width // 4, hidden_units // 4
    folds = width // both
    tall = rows_gu + rows_down * folds

    def body(*refs):
        saved_ref = refs[0]
        grad_refs = refs[1 : 1 + micro_count]
        hidden_refs = refs[1 + micro_count : 1 + 2 * micro_count]
        slot_refs = refs[1 + 2 * micro_count : 1 + 3 * micro_count]
        near_ref, ours_ref, down = refs[1 + 3 * micro_count :]
        mine = lax.axis_index("mirror")
        for c in range(folds):
            columns = slice(c * both, (c + 1) * both)
            down[c] = sum(
                dot_tn(hidden_refs[b][...], slot_refs[b][:, columns]) for b in range(micro_count)
            ).astype(BF16)
        for out_ref, place, j in ((near_ref, 0, 1), (near_ref, 1, 3), (ours_ref, 0, 0), (ours_ref, 1, 2)):
            at = pl.ds(pl.multiple_of((mine ^ j) * rows_gu, rows_gu), rows_gu)
            out_ref[place, :rows_gu, :] = sum(
                dot_tn(saved_ref[b * capacity : (b + 1) * capacity, at], grad_refs[b][...])
                for b in range(micro_count)
            ).astype(BF16)
            at = pl.ds(pl.multiple_of((mine ^ j) * rows_down, rows_down), rows_down)
            for c in range(folds):
                base = rows_gu + c * rows_down
                out_ref[place, base : base + rows_down, :] = down[c, at, :]

    return call(
        body,
        [saved, *grads, *hidden, *slots],
        [((2, tall, both), BF16)] * 2,
        flops=2 * micro_count * capacity * width * (both + hidden_units),
        scratch=[pltpu.VMEM((folds, hidden_units, both), BF16)],
    )


def near_sum(ours, near):
    def body(ours_ref, near_ref, out_ref):
        out_ref[...] = (ours_ref[1].astype(F32) + near_ref[1].astype(F32)).astype(BF16)

    return call(body, [ours, near], [(ours.shape[1:], BF16)])[0]


def final_sum(ours, near, far, rows_gu, rows_down):
    both = far.shape[1]
    folds = (far.shape[0] - rows_gu) // rows_down

    def body(ours_ref, near_ref, far_ref, gu_ref, down_ref):
        total = ours_ref[0].astype(F32) + near_ref[0].astype(F32) + far_ref[...].astype(F32)
        total = total.astype(BF16)
        gu_ref[...] = total[:rows_gu]
        for c in range(folds):
            base = rows_gu + c * rows_down
            down_ref[:, c * both : (c + 1) * both] = total[base : base + rows_down]

    shapes = [(rows_gu, both), (rows_down, both * folds)]
    return call(
        body,
        [ours, near, far],
        [(shape, BF16) for shape in shapes],
        out_specs=[copied_spec(shape) for shape in shapes],
    )


def gather_pieces(shards):
    far = [swap(shard, "mirror", 2) for shard in shards]
    near = [swap(shard, "mirror", 1) for shard in shards]
    corner = [swap(piece, "mirror", 1) for piece in far]
    return [list(pieces) for pieces in zip(shards, near, far, corner)]


def per_device(out_grad, gate_prob, dest_expert, dest_slot, x_saved, w_gate_up, w_down):
    n_expert = lax.axis_size("expert")
    micro_count = x_saved.shape[2]
    capacity = x_saved.shape[3]
    width = x_saved.shape[4]
    peer_slots = capacity // n_expert
    rows = out_grad.shape[3]
    small = n_expert <= 16
    permuted = [small and b % 2 == 0 for b in range(micro_count)]
    order = sorted(range(1, n_expert), key=lambda k: -k)

    def exchange(blocks, relative):
        if relative:
            moved = {0: blocks[0]}
            for k in order:
                moved[k] = swap(blocks[k], "expert", k)
            return [moved[k] for k in range(n_expert)]
        value = blocks[0]
        parts = value.reshape(n_expert, peer_slots, width)
        moved = lax.all_to_all(parts, "expert", split_axis=0, concat_axis=0, tiled=True)
        return [moved.reshape(value.shape)]

    grad, prob = out_grad[0, 0], gate_prob[0, 0]
    expert, slot = dest_expert[0, 0], dest_slot[0, 0]
    saved = x_saved[0, 0].reshape(micro_count * capacity, width)
    pieces_gu, pieces_down = gather_pieces([w_gate_up[0], w_down[0]])
    arrived = []
    after = None
    for b in range(micro_count):
        placed = place_rows(grad, prob, expert, slot, b, n_expert, peer_slots, permuted[b], after)
        after = placed[0]
        arrived.append(exchange(placed, permuted[b]))
    full_gu, full_down, gate_up = prepare(pieces_gu, pieces_down, saved)

    hidden_all, gu_all, slot_all, backs = [], [], [], []
    for b in range(micro_count):
        results = expert_rows(arrived[b], gate_up, full_gu, full_down, b, n_expert, permuted[b])
        count = len(arrived[b])
        gu_all.append(results[count])
        hidden_all.append(results[count + 1])
        slot_all.append(results[count + 2] if permuted[b] else arrived[b][0])
        backs.append(exchange(results[:count], permuted[b]))
    near, ours = weight_parts(saved, gu_all, hidden_all, slot_all)
    got_near = swap(near, "mirror", 1)
    pair = near_sum(ours, got_near)
    got_far = swap(pair, "mirror", 2)
    share_gu, share_down = final_sum(ours, got_near, got_far, w_gate_up.shape[1], w_down.shape[1])
    in_rows = None
    for b in range(micro_count):
        in_rows = unplace_rows(
            backs[b], expert, slot, b, n_expert, permuted[b], rows, in_rows, micro_count
        )
    return (in_rows[None, None], share_gu[None], share_down[None])


def solution(mesh):
    in_specs = (
        P("expert", "mirror", None, None, None),
        P("expert", "mirror", None, None),
        P("expert", "mirror", None, None),
        P("expert", "mirror", None, None),
        P("expert", "mirror", None, None, None),
        P("expert", "mirror", None),
        P("expert", "mirror", None),
    )
    out_specs = (
        P("expert", "mirror", None, None, None),
        P("expert", "mirror", None),
        P("expert", "mirror", None),
    )
    return jax.shard_map(
        per_device, mesh=mesh, in_specs=in_specs, out_specs=out_specs, check_vma=False
    )
```

```python
import jax
import jax.numpy as jnp
from jax import lax
from jax.experimental import pallas as pl
from jax.experimental.pallas import tpu as pltpu
from jax.sharding import PartitionSpec as P


BF16 = jnp.bfloat16
F32 = jnp.float32
VMEM_LIMIT = 12 * 1024 * 1024


def copied_spec(shape):
    zeros = (0,) * len(shape)
    return pl.BlockSpec(tuple(shape), lambda i: zeros)


def resident_spec():
    return pl.BlockSpec(memory_space=pltpu.VMEM)


def call(body, operands, out_shapes, flops=0, scratch=(), in_specs=None, out_specs=None, aliases=None, steps=1, exps=0):
    shapes = [jax.ShapeDtypeStruct(shape, dtype) for shape, dtype in out_shapes]
    moved = sum(v.size * v.dtype.itemsize for v in (*operands, *shapes))
    return pl.pallas_call(
        body,
        grid=(steps,),
        in_specs=in_specs or [resident_spec()] * len(operands),
        out_specs=out_specs or [resident_spec()] * len(shapes),
        out_shape=shapes,
        scratch_shapes=list(scratch),
        input_output_aliases=aliases or {},
        compiler_params=pltpu.CompilerParams(vmem_limit_bytes=VMEM_LIMIT),
        cost_estimate=pl.CostEstimate(flops=flops, bytes_accessed=moved, transcendentals=exps),
    )(*operands)


def dot_nt(left_side, right_side):
    return lax.dot_general(
        left_side, right_side, (((1,), (1,)), ((), ())), preferred_element_type=F32
    )


def dot_tn(left_side, right_side):
    return lax.dot_general(
        left_side, right_side, (((0,), (0,)), ((), ())), preferred_element_type=F32
    )


def silu_parts(values):
    sigmoid_vals = jax.nn.sigmoid(values)
    return (values * sigmoid_vals, sigmoid_vals * (1.0 + values * (1.0 - sigmoid_vals)))


def swap(value, axis, bit):
    size = lax.axis_size(axis)
    return lax.ppermute(value, axis, [(i, i ^ bit) for i in range(size)])


def as_column(row):
    count = row.shape[1]
    down = lax.broadcasted_iota(jnp.int32, (count, count), 0)
    across = lax.broadcasted_iota(jnp.int32, (count, count), 1)
    spread = jnp.broadcast_to(row, (count, count))
    return jnp.sum(jnp.where(down == across, spread, jnp.zeros_like(spread)), axis=1, keepdims=True)


STEP = 512
RELAYED = (0, 1)


def row_tables(refs, b, peer_slots, relative):
    if len(refs) == 3:
        prob_ref, expert_ref, slot_ref = refs
        prob = prob_ref[b : b + 1, :]
        position = expert_ref[b : b + 1, :] * peer_slots + slot_ref[b : b + 1, :]
    else:
        (both_ref,) = refs
        micro_count = both_ref.shape[0] // 2
        prob = both_ref[b : b + 1, :]
        position = both_ref[micro_count + b : micro_count + b + 1, :].astype(jnp.int32)
    if relative:
        position = position ^ (lax.axis_index("expert") * peer_slots)
    return prob, position


def place_rows(grads, tables, b, peers, peer_slots, relative):
    rows, width = grads.shape[1:]
    slot_count = peers * peer_slots
    count, block_rows = (peers, peer_slots) if relative else (1, slot_count)

    def body(*refs):
        out_refs, (grad_ref, *table_refs, sems) = refs[4 : 4 + count], refs[4 + count :]
        copies = [pltpu.make_async_copy(refs[0].at[b], grad_ref, sems.at[0])]
        copies += [
            pltpu.make_async_copy(refs[1 + i], table_refs[i], sems.at[1 + i]) for i in range(3)
        ]
        for copy in copies:
            copy.start()
        for copy in copies[1:]:
            copy.wait()
        prob, position = row_tables(table_refs, b, peer_slots, relative)
        slot_ids = lax.broadcasted_iota(jnp.int32, (slot_count, rows), 0)
        placing = jnp.where(slot_ids == position, 1.0, 0.0).astype(BF16)
        prob = as_column(prob)
        copies[0].wait()
        for start in range(0, width, STEP):
            columns = slice(start, start + STEP)
            weighted = (grad_ref[:, columns].astype(F32) * prob).astype(BF16)
            slots = jnp.dot(placing, weighted, preferred_element_type=F32).astype(BF16)
            for k in range(count):
                out_refs[k][:, columns] = slots[k * block_rows : (k + 1) * block_rows]

    return call(
        body,
        [pltpu.with_memory_space_constraint(v, pltpu.HBM) for v in (grads, *tables)],
        [((block_rows, width), BF16)] * count,
        flops=2 * slot_count * rows * width,
        in_specs=[pl.BlockSpec(memory_space=pltpu.HBM)] * 4,
        scratch=[
            pltpu.VMEM((rows, width), BF16),
            *[pltpu.VMEM(v.shape, v.dtype) for v in tables],
            pltpu.SemaphoreType.DMA((4,)),
        ],
    )


def prepare(pieces_gu, pieces_down, saved):
    rows_gu, both = pieces_gu[0].shape
    rows_down, width = pieces_down[0].shape
    count = len(pieces_gu)
    slots = saved.shape[0]

    def body(*refs):
        mine = lax.axis_index("mirror")
        saved_ref = refs[2 * count]
        gu_ref, down_ref, gate_up_ref = refs[2 * count + 1 :]
        total = None
        for j in range(count):
            at = pl.ds(pl.multiple_of((mine ^ j) * rows_gu, rows_gu), rows_gu)
            gu_ref[at, :] = refs[j][...]
            term = jnp.dot(saved_ref[:, at], refs[j][...], preferred_element_type=F32)
            total = term if total is None else total + term
            down = pl.ds(pl.multiple_of((mine ^ j) * rows_down, rows_down), rows_down)
            down_ref[down, :] = refs[count + j][...]
        gate_up_ref[...] = total

    return call(
        body,
        [*pieces_gu, *pieces_down, saved],
        [((count * rows_gu, both), BF16), ((count * rows_down, width), BF16), ((slots, both), F32)],
        flops=2 * slots * width * both,
    )


def expert_rows(arrived, gate_up, full_gu, full_down, b, n_expert, relative):
    both = gate_up.shape[1]
    hidden_units = both // 2
    width = full_gu.shape[0]
    count = len(arrived)
    peer_slots = arrived[0].shape[0] if relative else arrived[0].shape[0] // n_expert
    capacity = n_expert * peer_slots

    def body(*refs):
        blocks = refs[:count]
        gate_up_ref, gu_ref, down_ref = refs[count : count + 3]
        rows_refs = refs[count + 3 : 2 * count + 3]
        grad_ref, hidden_ref = refs[2 * count + 3 : 2 * count + 5]
        if relative:
            slots_ref, stage = refs[2 * count + 5 :]
            me = lax.axis_index("expert")
            spots = [
                pl.ds(pl.multiple_of((me ^ k) * peer_slots, peer_slots), peer_slots)
                for k in range(n_expert)
            ]
            for k in range(n_expert):
                slots_ref[spots[k], :] = blocks[k][...]
            unit_grad = dot_nt(slots_ref[...], down_ref[...])
        else:
            unit_grad = dot_nt(blocks[0][...], down_ref[...])
        mine = slice(b * capacity, (b + 1) * capacity)
        gate_part = gate_up_ref[mine, :hidden_units]
        up_part = gate_up_ref[mine, hidden_units:]
        activation, slope_term = silu_parts(gate_part)
        hidden_ref[...] = (activation * up_part).astype(BF16)
        grad_ref[:, :hidden_units] = (unit_grad * up_part * slope_term).astype(BF16)
        grad_ref[:, hidden_units:] = (unit_grad * activation).astype(BF16)
        for start in range(0, width, STEP):
            rows = dot_nt(grad_ref[...], gu_ref[start : start + STEP, :]).astype(BF16)
            if relative:
                stage[:, start : start + STEP] = rows
            else:
                rows_refs[0][:, start : start + STEP] = rows
        if relative:
            for k in range(n_expert):
                rows_refs[k][...] = stage[spots[k], :]

    out_shapes = [(arrived[0].shape, BF16)] * count
    out_shapes += [((capacity, both), BF16), ((capacity, hidden_units), BF16)]
    if relative:
        out_shapes.append(((capacity, width), BF16))
    operands = [*arrived, gate_up, full_gu, full_down]
    return call(
        body,
        operands,
        out_shapes,
        flops=2 * capacity * width * (both + hidden_units),
        exps=capacity * hidden_units,
        scratch=[pltpu.VMEM((capacity, width), BF16)] if relative else [],
    )


def collect_rows(blocks, tables, b, peers, peer_slots, relative, last=False, extras=(), previous=None):
    width = blocks[0].shape[1]
    micro_count, rows = tables[0].shape
    count = len(blocks)
    ahead = len(tables)
    block_rows = blocks[0].shape[0]
    slot_count = peers * peer_slots

    def body(*refs):
        block_refs = refs[ahead : ahead + count]
        extra_refs = refs[ahead + count : ahead + count + len(extras)]
        out_ref, stage = refs[-2:]
        position = as_column(row_tables(refs[:ahead], b, peer_slots, relative)[1])
        slot_ids = lax.broadcasted_iota(jnp.int32, (rows, slot_count), 1)
        taking = jnp.where(slot_ids == position, 1.0, 0.0).astype(BF16)
        for k in range(count):
            stage[k * block_rows : (k + 1) * block_rows, :] = block_refs[k][...]
        for start in range(0, width, STEP):
            columns = slice(start, start + STEP)
            taken = jnp.dot(taking, stage[:, columns], preferred_element_type=F32)
            for ref in extra_refs:
                taken = taken + ref[:, columns].astype(F32)
            if last:
                out_ref[0, :, columns] = taken.astype(BF16)
            else:
                out_ref[:, columns] = taken.astype(BF16)

    operands = [*tables, *blocks, *extras]
    in_specs = [resident_spec()] * len(operands)
    out_shape, out_specs, aliases = (rows, width), None, {}
    if last:
        out_shape = (micro_count, rows, width)
        out_specs = [pl.BlockSpec((1, rows, width), lambda i: (b, 0, 0))]
        if previous is not None:
            aliases = {len(operands): 0}
            operands.append(previous)
            in_specs.append(pl.BlockSpec(memory_space=pl.ANY))
    return call(
        body,
        operands,
        [(out_shape, BF16)],
        flops=2 * slot_count * rows * width,
        in_specs=in_specs,
        out_specs=out_specs,
        scratch=[pltpu.VMEM((slot_count, width), BF16)],
        aliases=aliases,
    )[0]


def weight_parts(saved, grads, hidden, slots):
    micro_count = len(grads)
    capacity, both = grads[0].shape
    hidden_units = hidden[0].shape[1]
    width = saved.shape[1]
    rows_gu, rows_down = width // 4, hidden_units // 4
    folds = width // both
    tall = rows_gu + rows_down * folds

    def body(*refs):
        saved_ref = refs[0]
        grad_refs = refs[1 : 1 + micro_count]
        hidden_refs = refs[1 + micro_count : 1 + 2 * micro_count]
        slot_refs = refs[1 + 2 * micro_count : 1 + 3 * micro_count]
        near_ref, ours_ref, down = refs[1 + 3 * micro_count :]
        mine = lax.axis_index("mirror")
        for c in range(folds):
            columns = slice(c * both, (c + 1) * both)
            down[c] = sum(
                dot_tn(hidden_refs[b][...], slot_refs[b][:, columns]) for b in range(micro_count)
            ).astype(BF16)
        for out_ref, place, j in ((near_ref, 0, 1), (near_ref, 1, 3), (ours_ref, 0, 0), (ours_ref, 1, 2)):
            at = pl.ds(pl.multiple_of((mine ^ j) * rows_gu, rows_gu), rows_gu)
            out_ref[place, :rows_gu, :] = sum(
                dot_tn(saved_ref[b * capacity : (b + 1) * capacity, at], grad_refs[b][...])
                for b in range(micro_count)
            ).astype(BF16)
            at = pl.ds(pl.multiple_of((mine ^ j) * rows_down, rows_down), rows_down)
            for c in range(folds):
                base = rows_gu + c * rows_down
                out_ref[place, base : base + rows_down, :] = down[c, at, :]

    return call(
        body,
        [saved, *grads, *hidden, *slots],
        [((2, tall, both), BF16)] * 2,
        flops=2 * micro_count * capacity * width * (both + hidden_units),
        scratch=[pltpu.VMEM((folds, hidden_units, both), BF16)],
    )


def near_sum(ours, near):
    def body(ours_ref, near_ref, out_ref):
        out_ref[...] = (ours_ref[1].astype(F32) + near_ref[1].astype(F32)).astype(BF16)

    return call(body, [ours, near], [(ours.shape[1:], BF16)])[0]


def final_sum(ours, near, far, rows_gu, rows_down):
    both = far.shape[1]
    folds = (far.shape[0] - rows_gu) // rows_down

    def body(ours_ref, near_ref, far_ref, gu_ref, down_ref):
        total = ours_ref[0].astype(F32) + near_ref[0].astype(F32) + far_ref[...].astype(F32)
        total = total.astype(BF16)
        gu_ref[...] = total[:rows_gu]
        for c in range(folds):
            base = rows_gu + c * rows_down
            down_ref[:, c * both : (c + 1) * both] = total[base : base + rows_down]

    shapes = [(rows_gu, both), (rows_down, both * folds)]
    return call(
        body,
        [ours, near, far],
        [(shape, BF16) for shape in shapes],
        out_specs=[copied_spec(shape) for shape in shapes],
    )


def gather_pieces(shards):
    far = [swap(shard, "mirror", 2) for shard in shards]
    near = [swap(shard, "mirror", 1) for shard in shards]
    corner = [swap(piece, "mirror", 1) for piece in far]
    return [list(pieces) for pieces in zip(shards, near, far, corner)]


def per_device(out_grad, gate_prob, dest_expert, dest_slot, x_saved, w_gate_up, w_down):
    n_expert = lax.axis_size("expert")
    micro_count = x_saved.shape[2]
    capacity = x_saved.shape[3]
    width = x_saved.shape[4]
    peer_slots = capacity // n_expert
    relay = n_expert in (4, 8, 16)
    half = n_expert // 2
    micros = range(micro_count)

    def send(value, bit):
        return swap(value, "expert", bit)

    def exchange(value):
        parts = value.reshape(n_expert, peer_slots, width)
        moved = lax.all_to_all(parts, "expert", split_axis=0, concat_axis=0, tiled=True)
        return moved.reshape(value.shape)

    grads = out_grad[0, 0]
    tables = [gate_prob[0, 0], dest_expert[0, 0], dest_slot[0, 0]]
    saved = x_saved[0, 0].reshape(micro_count * capacity, width)
    pieces_gu, pieces_down = gather_pieces([w_gate_up[0], w_down[0]])
    arrived = []
    order = [half, *range(half - 1, 0, -1), *range(half + 1, n_expert)]
    for b in micros:
        blocks = place_rows(grads, tables, b, n_expert, peer_slots, relay)
        if relay:
            turns = order if b == 0 else [*range(half, n_expert), *range(half - 1, 0, -1)]
            moved = {k: send(blocks[k], k) for k in turns}
            arrived.append([blocks[0]] + [moved[k] for k in range(1, n_expert)])
        else:
            arrived.append([exchange(blocks[0])])
    if relay:
        position = tables[1] * peer_slots + tables[2]
        far_tables = [send(jnp.concatenate([tables[0], position.astype(F32)]), half)]
    full_gu, full_down, gate_up = prepare(pieces_gu, pieces_down, saved)

    hidden_all, gu_all, slot_all, backs = [], [], [], []
    for b in micros:
        results = expert_rows(arrived[b], gate_up, full_gu, full_down, b, n_expert, relay)
        count = len(arrived[b])
        gu_all.append(results[count])
        hidden_all.append(results[count + 1])
        slot_all.append(results[count + 2] if relay else arrived[b][0])
        backs.append(results[:count])
    in_rows = None
    for b in micros:
        blocks, extras, peers = backs[b], [], n_expert
        if not relay:
            near = [exchange(blocks[0])]
        elif b not in RELAYED:
            moved = {k: send(blocks[k], k) for k in order}
            near = [blocks[0]] + [moved[k] for k in range(1, n_expert)]
        else:
            handed = [blocks[half]] + [send(blocks[half + k], k) for k in range(1, half)]
            near = [blocks[0]] + [send(blocks[k], k) for k in range(1, half)]
            others = collect_rows(handed, far_tables, b, half, peer_slots, True)
            extras = [send(others, half)]
            peers = half
        in_rows = collect_rows(near, tables, b, peers, peer_slots, relay, True, extras, in_rows)
    near, ours = weight_parts(saved, gu_all, hidden_all, slot_all)
    got_near = swap(near, "mirror", 1)
    pair = near_sum(ours, got_near)
    got_far = swap(pair, "mirror", 2)
    share_gu, share_down = final_sum(ours, got_near, got_far, w_gate_up.shape[1], w_down.shape[1])
    return (in_rows[None, None], share_gu[None], share_down[None])


def solution(mesh):
    in_specs = (
        P("expert", "mirror", None, None, None),
        P("expert", "mirror", None, None),
        P("expert", "mirror", None, None),
        P("expert", "mirror", None, None),
        P("expert", "mirror", None, None, None),
        P("expert", "mirror", None),
        P("expert", "mirror", None),
    )
    out_specs = (
        P("expert", "mirror", None, None, None),
        P("expert", "mirror", None),
        P("expert", "mirror", None),
    )
    return jax.shard_map(
        per_device, mesh=mesh, in_specs=in_specs, out_specs=out_specs, check_vma=False
    )
```

```python
import jax
import jax.numpy as jnp
from jax import lax
from jax.experimental import pallas as pl
from jax.experimental.pallas import tpu as pltpu
from jax.sharding import PartitionSpec as P


BF16 = jnp.bfloat16
F32 = jnp.float32
VMEM_LIMIT = 12 * 1024 * 1024


def copied_spec(shape):
    zeros = (0,) * len(shape)
    return pl.BlockSpec(tuple(shape), lambda i: zeros)


def resident_spec():
    return pl.BlockSpec(memory_space=pltpu.VMEM)


def call(body, operands, out_shapes, flops=0, scratch=(), in_specs=None, out_specs=None, aliases=None, steps=1, exps=0):
    shapes = [jax.ShapeDtypeStruct(shape, dtype) for shape, dtype in out_shapes]
    moved = sum(v.size * v.dtype.itemsize for v in (*operands, *shapes))
    return pl.pallas_call(
        body,
        grid=(steps,),
        in_specs=in_specs or [resident_spec()] * len(operands),
        out_specs=out_specs or [resident_spec()] * len(shapes),
        out_shape=shapes,
        scratch_shapes=list(scratch),
        input_output_aliases=aliases or {},
        compiler_params=pltpu.CompilerParams(vmem_limit_bytes=VMEM_LIMIT),
        cost_estimate=pl.CostEstimate(flops=flops, bytes_accessed=moved, transcendentals=exps),
    )(*operands)


def dot_nt(left_side, right_side):
    return lax.dot_general(
        left_side, right_side, (((1,), (1,)), ((), ())), preferred_element_type=F32
    )


def dot_tn(left_side, right_side):
    return lax.dot_general(
        left_side, right_side, (((0,), (0,)), ((), ())), preferred_element_type=F32
    )


def silu_parts(values):
    sigmoid_vals = jax.nn.sigmoid(values)
    return (values * sigmoid_vals, sigmoid_vals * (1.0 + values * (1.0 - sigmoid_vals)))


def swap(value, axis, bit):
    size = lax.axis_size(axis)
    return lax.ppermute(value, axis, [(i, i ^ bit) for i in range(size)])


def as_column(row):
    count = row.shape[1]
    down = lax.broadcasted_iota(jnp.int32, (count, count), 0)
    across = lax.broadcasted_iota(jnp.int32, (count, count), 1)
    spread = jnp.broadcast_to(row, (count, count))
    return jnp.sum(jnp.where(down == across, spread, jnp.zeros_like(spread)), axis=1, keepdims=True)


STEP = 512
RELAYED = (0, 1)
CUTS = 2


def row_tables(refs, b, peer_slots, relative):
    if len(refs) == 3:
        prob_ref, expert_ref, slot_ref = refs
        prob = prob_ref[b : b + 1, :]
        position = expert_ref[b : b + 1, :] * peer_slots + slot_ref[b : b + 1, :]
    else:
        (both_ref,) = refs
        micro_count = both_ref.shape[0] // 2
        prob = both_ref[b : b + 1, :]
        position = both_ref[micro_count + b : micro_count + b + 1, :].astype(jnp.int32)
    if relative:
        position = position ^ (lax.axis_index("expert") * peer_slots)
    return prob, position


def place_rows(grads, tables, b, peers, peer_slots, relative):
    rows, width = grads.shape[1:]
    slot_count = peers * peer_slots
    count, block_rows = (peers, peer_slots) if relative else (1, slot_count)

    def body(*refs):
        out_refs, (grad_ref, *table_refs, sems) = refs[4 : 4 + count], refs[4 + count :]
        copies = [pltpu.make_async_copy(refs[0].at[b], grad_ref, sems.at[0])]
        copies += [
            pltpu.make_async_copy(refs[1 + i], table_refs[i], sems.at[1 + i]) for i in range(3)
        ]
        for copy in copies:
            copy.start()
        for copy in copies[1:]:
            copy.wait()
        prob, position = row_tables(table_refs, b, peer_slots, relative)
        slot_ids = lax.broadcasted_iota(jnp.int32, (slot_count, rows), 0)
        placing = jnp.where(slot_ids == position, 1.0, 0.0).astype(BF16)
        prob = as_column(prob)
        copies[0].wait()
        for start in range(0, width, STEP):
            columns = slice(start, start + STEP)
            weighted = (grad_ref[:, columns].astype(F32) * prob).astype(BF16)
            slots = jnp.dot(placing, weighted, preferred_element_type=F32).astype(BF16)
            for k in range(count):
                out_refs[k][:, columns] = slots[k * block_rows : (k + 1) * block_rows]

    return call(
        body,
        [pltpu.with_memory_space_constraint(v, pltpu.HBM) for v in (grads, *tables)],
        [((block_rows, width), BF16)] * count,
        flops=2 * slot_count * rows * width,
        in_specs=[pl.BlockSpec(memory_space=pltpu.HBM)] * 4,
        scratch=[
            pltpu.VMEM((rows, width), BF16),
            *[pltpu.VMEM(v.shape, v.dtype) for v in tables],
            pltpu.SemaphoreType.DMA((4,)),
        ],
    )


def prepare(pieces_gu, pieces_down, saved):
    rows_gu, both = pieces_gu[0].shape
    rows_down, width = pieces_down[0].shape
    count = len(pieces_gu)
    slots = saved.shape[0]

    def body(*refs):
        mine = lax.axis_index("mirror")
        saved_ref = refs[2 * count]
        gu_ref, down_ref, gate_up_ref = refs[2 * count + 1 :]
        total = None
        for j in range(count):
            at = pl.ds(pl.multiple_of((mine ^ j) * rows_gu, rows_gu), rows_gu)
            gu_ref[at, :] = refs[j][...]
            term = jnp.dot(saved_ref[:, at], refs[j][...], preferred_element_type=F32)
            total = term if total is None else total + term
            down = pl.ds(pl.multiple_of((mine ^ j) * rows_down, rows_down), rows_down)
            down_ref[down, :] = refs[count + j][...]
        gate_up_ref[...] = total

    return call(
        body,
        [*pieces_gu, *pieces_down, saved],
        [((count * rows_gu, both), BF16), ((count * rows_down, width), BF16), ((slots, both), F32)],
        flops=2 * slots * width * both,
    )


def expert_rows(arrived, gate_up, full_gu, full_down, b, n_expert, relative):
    both = gate_up.shape[1]
    hidden_units = both // 2
    width = full_gu.shape[0]
    count = len(arrived)
    peer_slots = arrived[0].shape[0] if relative else arrived[0].shape[0] // n_expert
    capacity = n_expert * peer_slots

    def body(*refs):
        blocks = refs[:count]
        gate_up_ref, gu_ref, down_ref = refs[count : count + 3]
        rows_refs = refs[count + 3 : 2 * count + 3]
        grad_ref, hidden_ref = refs[2 * count + 3 : 2 * count + 5]
        if relative:
            slots_ref, stage = refs[2 * count + 5 :]
            me = lax.axis_index("expert")
            spots = [
                pl.ds(pl.multiple_of((me ^ k) * peer_slots, peer_slots), peer_slots)
                for k in range(n_expert)
            ]
            for k in range(n_expert):
                slots_ref[spots[k], :] = blocks[k][...]
            unit_grad = dot_nt(slots_ref[...], down_ref[...])
        else:
            unit_grad = dot_nt(blocks[0][...], down_ref[...])
        mine = slice(b * capacity, (b + 1) * capacity)
        gate_part = gate_up_ref[mine, :hidden_units]
        up_part = gate_up_ref[mine, hidden_units:]
        activation, slope_term = silu_parts(gate_part)
        hidden_ref[...] = (activation * up_part).astype(BF16)
        grad_ref[:, :hidden_units] = (unit_grad * up_part * slope_term).astype(BF16)
        grad_ref[:, hidden_units:] = (unit_grad * activation).astype(BF16)
        for start in range(0, width, STEP):
            rows = dot_nt(grad_ref[...], gu_ref[start : start + STEP, :]).astype(BF16)
            if relative:
                stage[:, start : start + STEP] = rows
            else:
                rows_refs[0][:, start : start + STEP] = rows
        if relative:
            for k in range(n_expert):
                rows_refs[k][...] = stage[spots[k], :]

    out_shapes = [(arrived[0].shape, BF16)] * count
    out_shapes += [((capacity, both), BF16), ((capacity, hidden_units), BF16)]
    if relative:
        out_shapes.append(((capacity, width), BF16))
    operands = [*arrived, gate_up, full_gu, full_down]
    return call(
        body,
        operands,
        out_shapes,
        flops=2 * capacity * width * (both + hidden_units),
        exps=capacity * hidden_units,
        scratch=[pltpu.VMEM((capacity, width), BF16)] if relative else [],
    )


def collect_rows(blocks, tables, b, peers, peer_slots, relative, parts=1, last=False, extras=(), previous=None):
    width = blocks[0].shape[1]
    micro_count, rows = tables[0].shape
    if len(tables) == 1:
        micro_count //= 2
    count = len(blocks)
    ahead = len(tables)
    block_rows = blocks[0].shape[0]
    slot_count = peers * peer_slots
    part_width = width // parts

    def body(*refs):
        block_refs = refs[ahead : ahead + count]
        extra_refs = refs[ahead + count : ahead + count + len(extras)]
        out_refs, stage = refs[-1 - parts : -1], refs[-1]
        position = as_column(row_tables(refs[:ahead], b, peer_slots, relative)[1])
        slot_ids = lax.broadcasted_iota(jnp.int32, (rows, slot_count), 1)
        taking = jnp.where(slot_ids == position, 1.0, 0.0).astype(BF16)
        for k in range(count):
            stage[k * block_rows : (k + 1) * block_rows, :] = block_refs[k][...]
        for start in range(0, width, STEP):
            columns = slice(start, start + STEP)
            taken = jnp.dot(taking, stage[:, columns], preferred_element_type=F32)
            if extras:
                extra_width = width // len(extras)
                offset = start % extra_width
                taken = taken + extra_refs[start // extra_width][:, offset : offset + STEP].astype(F32)
            if last:
                out_refs[0][0, :, columns] = taken.astype(BF16)
            else:
                offset = start % part_width
                out_refs[start // part_width][:, offset : offset + STEP] = taken.astype(BF16)

    operands = [*tables, *blocks, *extras]
    in_specs = [resident_spec()] * len(operands)
    out_shape, out_specs, aliases = (rows, part_width), None, {}
    if last:
        out_shape = (micro_count, rows, width)
        out_specs = [pl.BlockSpec((1, rows, width), lambda i: (b, 0, 0))]
        if previous is not None:
            aliases = {len(operands): 0}
            operands.append(previous)
            in_specs.append(pl.BlockSpec(memory_space=pl.ANY))
    return call(
        body,
        operands,
        [(out_shape, BF16)] * parts,
        flops=2 * slot_count * rows * width,
        in_specs=in_specs,
        out_specs=out_specs,
        scratch=[pltpu.VMEM((slot_count, width), BF16)],
        aliases=aliases,
    )


def weight_parts(saved, grads, hidden, slots):
    micro_count = len(grads)
    capacity, both = grads[0].shape
    hidden_units = hidden[0].shape[1]
    width = saved.shape[1]
    rows_gu, rows_down = width // 4, hidden_units // 4
    folds = width // both
    tall = rows_gu + rows_down * folds

    def body(*refs):
        saved_ref = refs[0]
        grad_refs = refs[1 : 1 + micro_count]
        hidden_refs = refs[1 + micro_count : 1 + 2 * micro_count]
        slot_refs = refs[1 + 2 * micro_count : 1 + 3 * micro_count]
        near_ref, ours_ref, down = refs[1 + 3 * micro_count :]
        mine = lax.axis_index("mirror")
        for c in range(folds):
            columns = slice(c * both, (c + 1) * both)
            down[c] = sum(
                dot_tn(hidden_refs[b][...], slot_refs[b][:, columns]) for b in range(micro_count)
            ).astype(BF16)
        for out_ref, place, j in ((near_ref, 0, 1), (near_ref, 1, 3), (ours_ref, 0, 0), (ours_ref, 1, 2)):
            at = pl.ds(pl.multiple_of((mine ^ j) * rows_gu, rows_gu), rows_gu)
            out_ref[place, :rows_gu, :] = sum(
                dot_tn(saved_ref[b * capacity : (b + 1) * capacity, at], grad_refs[b][...])
                for b in range(micro_count)
            ).astype(BF16)
            at = pl.ds(pl.multiple_of((mine ^ j) * rows_down, rows_down), rows_down)
            for c in range(folds):
                base = rows_gu + c * rows_down
                out_ref[place, base : base + rows_down, :] = down[c, at, :]

    return call(
        body,
        [saved, *grads, *hidden, *slots],
        [((2, tall, both), BF16)] * 2,
        flops=2 * micro_count * capacity * width * (both + hidden_units),
        scratch=[pltpu.VMEM((folds, hidden_units, both), BF16)],
    )


def near_sum(ours, near):
    def body(ours_ref, near_ref, out_ref):
        out_ref[...] = (ours_ref[1].astype(F32) + near_ref[1].astype(F32)).astype(BF16)

    return call(body, [ours, near], [(ours.shape[1:], BF16)])[0]


def final_sum(ours, near, far, rows_gu, rows_down):
    both = far.shape[1]
    folds = (far.shape[0] - rows_gu) // rows_down

    def body(ours_ref, near_ref, far_ref, gu_ref, down_ref):
        total = ours_ref[0].astype(F32) + near_ref[0].astype(F32) + far_ref[...].astype(F32)
        total = total.astype(BF16)
        gu_ref[...] = total[:rows_gu]
        for c in range(folds):
            base = rows_gu + c * rows_down
            down_ref[:, c * both : (c + 1) * both] = total[base : base + rows_down]

    shapes = [(rows_gu, both), (rows_down, both * folds)]
    return call(
        body,
        [ours, near, far],
        [(shape, BF16) for shape in shapes],
        out_specs=[copied_spec(shape) for shape in shapes],
    )


def gather_pieces(shards):
    far = [swap(shard, "mirror", 2) for shard in shards]
    near = [swap(shard, "mirror", 1) for shard in shards]
    corner = [swap(piece, "mirror", 1) for piece in far]
    return [list(pieces) for pieces in zip(shards, near, far, corner)]


def per_device(out_grad, gate_prob, dest_expert, dest_slot, x_saved, w_gate_up, w_down):
    n_expert = lax.axis_size("expert")
    micro_count = x_saved.shape[2]
    capacity = x_saved.shape[3]
    width = x_saved.shape[4]
    peer_slots = capacity // n_expert
    relay = n_expert in (4, 8, 16)
    half = n_expert // 2
    micros = range(micro_count)

    def send(value, bit):
        return swap(value, "expert", bit)

    def exchange(value):
        parts = value.reshape(n_expert, peer_slots, width)
        moved = lax.all_to_all(parts, "expert", split_axis=0, concat_axis=0, tiled=True)
        return moved.reshape(value.shape)

    grads = out_grad[0, 0]
    tables = [gate_prob[0, 0], dest_expert[0, 0], dest_slot[0, 0]]
    saved = x_saved[0, 0].reshape(micro_count * capacity, width)
    pieces_gu, pieces_down = gather_pieces([w_gate_up[0], w_down[0]])
    arrived = []
    order = [half, *range(half - 1, 0, -1), *range(half + 1, n_expert)]
    for b in micros:
        blocks = place_rows(grads, tables, b, n_expert, peer_slots, relay)
        if relay:
            turns = order if b == 0 else [1, 4, 5, 6, 7, 2, 3]
            moved = {k: send(blocks[k], k) for k in turns}
            arrived.append([blocks[0]] + [moved[k] for k in range(1, n_expert)])
        else:
            arrived.append([exchange(blocks[0])])
    if relay:
        position = tables[1] * peer_slots + tables[2]
        far_tables = [send(jnp.concatenate([tables[0], position.astype(F32)]), half)]
    full_gu, full_down, gate_up = prepare(pieces_gu, pieces_down, saved)

    hidden_all, gu_all, slot_all, backs = [], [], [], []
    for b in micros:
        results = expert_rows(arrived[b], gate_up, full_gu, full_down, b, n_expert, relay)
        count = len(arrived[b])
        gu_all.append(results[count])
        hidden_all.append(results[count + 1])
        slot_all.append(results[count + 2] if relay else arrived[b][0])
        backs.append(results[:count])
    in_rows = None
    for b in micros:
        blocks, extras, peers = backs[b], [], n_expert
        if not relay:
            near = [exchange(blocks[0])]
        elif b not in RELAYED:
            moved = {k: send(blocks[k], k) for k in order}
            near = [blocks[0]] + [moved[k] for k in range(1, n_expert)]
        else:
            handed = [blocks[half]] + [send(blocks[half + k], k) for k in range(1, half)]
            near = [blocks[0]] + [send(blocks[k], k) for k in range(1, half)]
            parts = CUTS if b + 1 < micro_count else 1
            others = collect_rows(handed, far_tables, b, half, peer_slots, True, parts)
            extras = [send(others[i], half) for i in range(parts)]
            peers = half
        in_rows = collect_rows(
            near, tables, b, peers, peer_slots, relay, 1, True, extras, in_rows
        )[0]
    near, ours = weight_parts(saved, gu_all, hidden_all, slot_all)
    got_near = swap(near, "mirror", 1)
    pair = near_sum(ours, got_near)
    got_far = swap(pair, "mirror", 2)
    share_gu, share_down = final_sum(ours, got_near, got_far, w_gate_up.shape[1], w_down.shape[1])
    return (in_rows[None, None], share_gu[None], share_down[None])


def solution(mesh):
    in_specs = (
        P("expert", "mirror", None, None, None),
        P("expert", "mirror", None, None),
        P("expert", "mirror", None, None),
        P("expert", "mirror", None, None),
        P("expert", "mirror", None, None, None),
        P("expert", "mirror", None),
        P("expert", "mirror", None),
    )
    out_specs = (
        P("expert", "mirror", None, None, None),
        P("expert", "mirror", None),
        P("expert", "mirror", None),
    )
    return jax.shard_map(
        per_device, mesh=mesh, in_specs=in_specs, out_specs=out_specs, check_vma=False
    )
```
